32 devices in a mesh: seq: 8 (over z, x), head: 4 (over y, core).
Axes of the slice: x: 2, y: 2, z: 4, core: 2. Of those that a mesh axis runs over, the one named last changes fastest.
Arguments:
- hidden: bfloat16 [1, 2048, 1024], P(None, 'seq'), may hold values from -6 to 6
- cotangent: bfloat16 [1, 2048, 1024], P(None, 'seq'), may hold values from -6 to 6
- pre_gain: float32 [1024], replicated, may hold values from 0.5 to 1.5
- w_zx: bfloat16 [1024, 2, 2048], P(None, None, 'head'), may hold values from -0.1875 to 0.1875
- w_bc: bfloat16 [1024, 256], replicated, may hold values from -0.1875 to 0.1875
- w_dt: bfloat16 [1024, 32], P(None, 'head'), may hold values from -0.1875 to 0.1875
- conv_x_w: float32 [4, 2048], P(None, 'head'), may hold values from -0.5 to 0.5
- conv_x_b: float32 [2048], P('head'), may hold values from -0.5 to 0.5
- conv_bc_w: float32 [4, 256], replicated, may hold values from -0.5 to 0.5
- conv_bc_b: float32 [256], replicated, may hold values from -0.5 to 0.5
- dt_bias: float32 [32], P('head'), may hold values from -4.5 to -2.5
- a_log: float32 [32], P('head'), as said below
- d_skip: float32 [32], P('head'), may hold values from 0.5 to 1.5
- gate_gain: float32 [2048], P('head'), may hold values from 0.5 to 1.5
- w_out: bfloat16 [2048, 1024], P('head'), may hold values from -0.125 to 0.125
Outputs:
- output: bfloat16 [1, 2048, 1024], P(None, 'seq')
- grad_hidden: float32 [1, 2048, 1024], P(None, 'seq')
- grad_pre_gain: float32 [1024], replicated
- grad_w_zx: float32 [1024, 2, 2048], P('seq', None, 'head')
- grad_w_bc: float32 [1024, 256], P('seq')
- grad_w_dt: float32 [1024, 32], P('seq', 'head')
- grad_conv_x_w: float32 [4, 2048], P(None, 'head')
- grad_conv_x_b: float32 [2048], P('head')
- grad_conv_bc_w: float32 [4, 256], replicated
- grad_conv_bc_b: float32 [256], replicated
- grad_dt_bias: float32 [32], P('head')
- grad_a_log: float32 [32], P('head')
- grad_d_skip: float32 [32], P('head')
- grad_gate_gain: float32 [2048], P('head')
- grad_w_out: float32 [2048, 1024], P('head', 'seq')
The draws below stay inside these ranges and needn't reach their ends.
Inputs may be any that keep to these rules, and one draw needn't show every extreme that they name: Each head's decay rate exp(a_log) lies between 2.4 / 2048 and 2.
All inputs are finite; a program needn't handle non-finite values.
Results may differ from the reference program's by a relative error of at most 0.003.
The reference program's roundings to bfloat16 on the way count: a program that leaves them out, or rounds other values in their place, can miss the bound.
Values may be sent and summed in bfloat16 or wider, within the bound.
A program may use at most 128 MiB of HBM per device.

```python
import math
import jax
import jax.numpy as jnp
from jax import lax

D = 1024
DI = 2048
H = 32
P_SIZE = 64
NS = 128
KW = 4
BLOCK = 256
SEQS = 1
LENGTH = 2048


def draw_a_log(key, part):
    first, second, third = jax.random.split(key, 3)
    chooser = jax.random.uniform(first, (H,))
    share = 0.5
    fast_rate = jnp.exp(jax.random.uniform(second, (H,), minval=math.log(0.5), maxval=math.log(2.0)))
    slow_rate = 8.0 / LENGTH * jnp.exp(jax.random.uniform(third, (H,), minval=math.log(0.3), maxval=math.log(1.5)))
    return jnp.log(jnp.where(chooser < share, fast_rate, slow_rate)).astype(jnp.float32)


def steps_of(stream_key, dims, shards, low, high):
    factor_of, own = 1.0, jax.random.fold_in(stream_key, 6)
    for dim, parts in shards:
        heights = jnp.exp(jax.random.uniform(jax.random.fold_in(own, dim), (parts,), jnp.float32, low / len(shards), high / len(shards)))
        factor_of = factor_of * jnp.repeat(heights, dims[dim] // parts).reshape([-1 if axis == dim else 1 for axis in range(len(dims))])
    return factor_of


def gaussian(key, shape, scale, bound, cuts=(), dtype=jnp.bfloat16):
    level = steps_of(key, shape, cuts, -0.22, 0.18) if cuts else 1.0
    result = jax.random.normal(key, shape, jnp.float32) * scale * level
    return jnp.minimum(jnp.maximum(result, -bound), bound).astype(dtype)


def setup_inputs(seed: int = 0) -> dict:
    arg_keys = jax.random.split(jax.random.key(seed), 16)
    hidden = gaussian(arg_keys[0], (SEQS, LENGTH, D), 1.0, 6.0, ((1, 8),))
    cotangent = gaussian(arg_keys[1], (SEQS, LENGTH, D), 1.0, 6.0, ((1, 8),))
    pre_gain = jnp.clip(1.0 + 0.1 * jax.random.normal(arg_keys[2], (D,), jnp.float32), 0.5, 1.5)
    w_zx = gaussian(arg_keys[3], (D, 2, DI), D ** -0.5, 0.1875, ((2, 4),))
    w_bc = gaussian(arg_keys[4], (D, 2 * NS), D ** -0.5, 0.1875)
    w_dt = gaussian(arg_keys[5], (D, H), D ** -0.5, 0.1875, ((1, 4),))
    conv_x_w = jnp.clip(jax.random.uniform(arg_keys[6], (KW, DI), jnp.float32, -0.5, 0.5) * steps_of(arg_keys[6], (KW, DI), ((1, 4),), -0.4, 0.0), -0.5, 0.5)
    conv_x_b = jnp.clip(jax.random.uniform(arg_keys[7], (DI,), jnp.float32, -0.5, 0.5) * steps_of(arg_keys[7], (DI,), ((0, 4),), -0.4, 0.0), -0.5, 0.5)
    conv_bc_w = jnp.clip(jax.random.uniform(arg_keys[8], (KW, 2 * NS), jnp.float32, -0.5, 0.5), -0.5, 0.5)
    conv_bc_b = jnp.clip(jax.random.uniform(arg_keys[9], (2 * NS,), jnp.float32, -0.5, 0.5), -0.5, 0.5)
    dt_bias = jnp.clip(-4.5 + 2.0 * jax.random.uniform(arg_keys[10], (H,), jnp.float32) ** steps_of(arg_keys[10], (H,), ((0, 4),), -0.2, 0.2), -4.5, -2.5)
    a_log = draw_a_log(jax.random.fold_in(arg_keys[15], 71), 0)
    d_skip = jnp.clip(0.5 + 1.0 * jax.random.uniform(arg_keys[12], (H,), jnp.float32) ** steps_of(arg_keys[12], (H,), ((0, 4),), -0.2, 0.2), 0.5, 1.5)
    gate_gain = jnp.clip(1.0 + 0.1 * jax.random.normal(arg_keys[13], (DI,), jnp.float32), 0.5, 1.5)
    w_out = gaussian(arg_keys[14], (DI, D), DI ** -0.5, 0.125, ((0, 4),))
    return dict(hidden=hidden, cotangent=cotangent, pre_gain=pre_gain, w_zx=w_zx, w_bc=w_bc, w_dt=w_dt, conv_x_w=conv_x_w, conv_x_b=conv_x_b, conv_bc_w=conv_bc_w, conv_bc_b=conv_bc_b, dt_bias=dt_bias, a_log=a_log, d_skip=d_skip, gate_gain=gate_gain, w_out=w_out)


@jax.custom_vjp
def low(v):
    return lax.optimization_barrier(v.astype(jnp.bfloat16)).astype(jnp.float32)

@jax.custom_vjp
def low_back(v):
    return v

def low_keep(v):
    return (low(v), None)

def low_pass(kept, grad):
    return (grad,)

def back_keep(v):
    return (v, None)

def back_low(kept, grad):
    return (low(grad),)
low.defvjp(low_keep, low_pass)
low_back.defvjp(back_keep, back_low)
EPSILON = 1e-05
HIGHEST = lax.Precision.HIGHEST

def causal_conv(values, weight, offset_b):
    length = values.shape[0]
    padded = jnp.pad(values, ((KW - 1, 0), (0, 0)))
    summed = offset_b + weight[0] * padded[0:length]
    for offset in range(1, KW):
        summed = summed + weight[offset] * padded[offset:offset + length]
    return summed

def block_step(carried, inputs):
    x_heads, b_mat, c_mat, deltas, log_decay = inputs
    cumulative = jnp.cumsum(log_decay, axis=0)
    scores = jnp.dot(c_mat, b_mat.T, precision=HIGHEST)
    row_ids = lax.broadcasted_iota(jnp.int32, (BLOCK, BLOCK), 0)
    column_ids = lax.broadcasted_iota(jnp.int32, (BLOCK, BLOCK), 1)
    causal = (row_ids >= column_ids)[:, :, None]
    spread = cumulative[:, None, :] - cumulative[None, :, :]
    decays = jnp.where(causal, jnp.exp(jnp.where(causal, spread, 0.0)), 0.0)
    weights = scores[:, :, None] * decays * deltas[None, :, :]
    inside = jnp.einsum('tsh,shp->thp', weights, x_heads, precision=HIGHEST)
    outside = jnp.exp(cumulative)[:, :, None] * jnp.einsum('tn,hpn->thp', c_mat, carried, precision=HIGHEST)
    tail_w = jnp.exp(cumulative[-1][None, :] - cumulative) * deltas
    local_state = jnp.einsum('shp,sn->hpn', tail_w[:, :, None] * x_heads, b_mat, precision=HIGHEST)
    carried = jnp.exp(cumulative[-1])[:, None, None] * carried + local_state
    return (carried, inside + outside)

def sequence(residual, params):
    pre_gain, w_zx, w_bc, w_dt, conv_x_w, conv_x_b, conv_bc_w, conv_bc_b, dt_bias, a_log, d_skip, gate_gain, w_out = params
    length = residual.shape[0]
    in_rstd = lax.rsqrt(lax.optimization_barrier(jnp.mean(residual * residual, axis=-1, keepdims=True)) + EPSILON)
    normed_in = low(residual * in_rstd * pre_gain)
    projected = low_back(jnp.einsum('ld,dke->lke', normed_in, w_zx, precision=HIGHEST))
    gating = projected[:, 0]
    conv_in = low(projected[:, 1])
    bc_in = low(low_back(jnp.dot(normed_in, w_bc, precision=HIGHEST)))
    dt_raw = low_back(jnp.dot(normed_in, w_dt, precision=HIGHEST))
    x_heads = low(jax.nn.silu(causal_conv(conv_in, conv_x_w, conv_x_b))).reshape(length, H, P_SIZE)
    bc_post = jax.nn.silu(causal_conv(bc_in, conv_bc_w, conv_bc_b))
    b_mat = low(bc_post[:, :NS])
    c_mat = low(bc_post[:, NS:])
    deltas = jax.nn.softplus(dt_raw + dt_bias)
    log_decay = deltas * -jnp.exp(a_log)
    block_count = length // BLOCK
    inputs = (x_heads.reshape(block_count, BLOCK, H, P_SIZE), b_mat.reshape(block_count, BLOCK, NS), c_mat.reshape(block_count, BLOCK, NS), deltas.reshape(block_count, BLOCK, H), log_decay.reshape(block_count, BLOCK, H))
    initial = jnp.zeros((H, P_SIZE, NS), jnp.float32)
    _, mixed = lax.scan(jax.checkpoint(block_step), initial, inputs)
    ssd_out = mixed.reshape(length, H, P_SIZE) + d_skip[None, :, None] * x_heads
    gated = ssd_out.reshape(length, DI) * jax.nn.silu(gating)
    gate_rstd = lax.rsqrt(lax.optimization_barrier(jnp.mean(gated * gated, axis=-1, keepdims=True)) + EPSILON)
    normed_out = low(gated * gate_rstd * gate_gain)
    return residual + jnp.dot(normed_out, w_out, precision=HIGHEST)

def layer(hidden, params):

    def one_sequence(sequence_in):
        return sequence(sequence_in, params)
    return lax.map(jax.checkpoint(one_sequence), hidden)

def reference(hidden, cotangent, pre_gain, w_zx, w_bc, w_dt, conv_x_w, conv_x_b, conv_bc_w, conv_bc_b, dt_bias, a_log, d_skip, gate_gain, w_out):
    params = tuple((entry.astype(jnp.float32) for entry in (pre_gain, w_zx, w_bc, w_dt, conv_x_w, conv_x_b, conv_bc_w, conv_bc_b, dt_bias, a_log, d_skip, gate_gain, w_out)))
    output, pullback = jax.vjp(layer, hidden.astype(jnp.float32), params)
    grad_hidden, gradients = pullback(cotangent.astype(jnp.float32))
    return (output.astype(jnp.bfloat16), grad_hidden, gradients[0], gradients[1], gradients[2], gradients[3], gradients[4], gradients[5], gradients[6], gradients[7], gradients[8], gradients[9], gradients[10], gradients[11], gradients[12])
```

```python
import functools

import jax
import jax.numpy as jnp
from jax import lax
from jax.experimental import pallas as pl
from jax.experimental.pallas import tpu as pltpu
from jax.sharding import PartitionSpec as P

MESH = pl.DeviceIdType.MESH
VMEM = pltpu.VMEM
DMA = pltpu.SemaphoreType.DMA
IN_VMEM = pl.BlockSpec(memory_space=pltpu.VMEM)

EPSILON = 1e-05
HIGHEST = lax.Precision.HIGHEST


def from_behind(value, axis, by):
    peers = lax.axis_size(axis)
    pairs = [(i, i + by) for i in range(peers) if 0 <= i + by < peers]
    return lax.ppermute(value, axis, pairs)


def kept_low(values):
    return lax.optimization_barrier(values.astype(jnp.bfloat16)).astype(jnp.float32)


def silu_slope(values):
    sigmoid = jax.nn.sigmoid(values)
    return sigmoid * (1.0 + values * (1.0 - sigmoid))


def conv_apply(extended, weight, offset_b, length):
    summed = offset_b + weight[0] * extended[:, 0:length]
    for offset in range(1, weight.shape[0]):
        summed = summed + weight[offset] * extended[:, offset : offset + length]
    return summed


def conv_reverse(extended, weight, grad_pre, length):
    conv_reach = weight.shape[0] - 1
    grad_weight = jnp.stack(
        [
            jnp.sum(grad_pre * extended[:, offset : offset + length], axis=(0, 1))
            for offset in range(conv_reach + 1)
        ],
        0,
    )
    grad_offset = jnp.sum(grad_pre, axis=(0, 1))
    grad_ext = jnp.pad(weight[0] * grad_pre, ((0, 0), (0, conv_reach), (0, 0)))
    for offset in range(1, conv_reach + 1):
        grad_ext = grad_ext + jnp.pad(
            weight[offset] * grad_pre, ((0, 0), (offset, conv_reach - offset), (0, 0))
        )
    return (grad_weight, grad_offset, grad_ext)


def scan_kernel(
    peers, backward, s_ref, d_ref, out_ref,
    part_s, part_d, carry_in, carry_out, back_out, back_in, send, recv,
):
    me = lax.axis_index("seq")
    place = peers - 1 - me if backward else me
    pairs = peers // 2
    k, j = place // 2, place % 2
    hh = part_s.shape[0]

    def device(position):
        return {"seq": peers - 1 - position if backward else position}

    partner = device(place + 1 - 2 * j)
    barrier = pltpu.get_barrier_semaphore()
    for to in (partner, device((place + 2) % peers), device((place + peers - 2) % peers)):
        pl.semaphore_signal(barrier, inc=1, device_id=to, device_id_type=MESH)
    pl.semaphore_wait(barrier, 3)

    def remote(source, target, slot, to):
        return pltpu.make_async_remote_copy(
            src_ref=source, dst_ref=target, send_sem=send.at[slot], recv_sem=recv.at[slot],
            device_id=to, device_id_type=MESH,
        )

    theirs, mine = pl.ds((1 - j) * hh, hh), pl.ds(j * hh, hh)
    give_s = remote(s_ref.at[theirs], part_s, 0, partner)
    give_d = remote(d_ref.at[theirs], part_d, 1, partner)
    give_s.start()
    give_d.start()
    give_s.wait()
    give_d.wait()
    early = j == 0
    own_s, own_d = s_ref[mine], d_ref[mine]
    s0 = jnp.where(early, own_s, part_s[...])
    s1 = jnp.where(early, part_s[...], own_s)
    d0 = jnp.where(early, own_d, part_d[...])
    d1 = jnp.where(early, part_d[...], own_d)
    onward = remote(carry_out, carry_in, 2, device((place + 2) % peers))

    @pl.when(k == 0)
    def _():
        carry_in[...] = jnp.zeros_like(carry_in)

    @pl.when(k > 0)
    def _():
        onward.wait_recv()

    before = carry_in[...]
    middle = d0 * before + s0

    @pl.when(k < pairs - 1)
    def _():
        carry_out[...] = d1 * middle + s1
        onward.start()

    back_out[...] = jnp.where(early, middle, before)
    back = remote(back_out, back_in, 3, partner)
    back.start()
    out_ref[mine] = jnp.where(early, before, middle)
    back.wait()
    out_ref[theirs] = back_in[...]

    @pl.when(k < pairs - 1)
    def _():
        onward.wait_send()


def state_scan(decay, state, backward):
    heads, size, states = state.shape
    hh = heads // 2
    half = VMEM((hh, size, states), jnp.float32)
    wide = jnp.broadcast_to(decay[:, None, None], (heads, 1, states))
    return pl.pallas_call(
        functools.partial(scan_kernel, lax.axis_size("seq"), backward),
        out_shape=jax.ShapeDtypeStruct(state.shape, jnp.float32),
        in_specs=[IN_VMEM] * 2,
        out_specs=IN_VMEM,
        scratch_shapes=[
            half, VMEM((hh, 1, states), jnp.float32), half, half, half, half, DMA((4,)), DMA((4,)),
        ],
        compiler_params=pltpu.CompilerParams(
            collective_id=2 if backward else 1, has_side_effects=True
        ),
        cost_estimate=pl.CostEstimate(
            flops=10**7, bytes_accessed=5 * 10**7, transcendentals=0
        ),
        name="scan_back" if backward else "scan_ahead",
    )(state, wide)


def sums_kernel(
    peers, groups, side_at,
    rows_ref, right_ref, left_ref, cols_ref, minor_ref, back_ref, mix_ref, hidden_ref,
    a_ref, b_ref, m_ref, g_ref, n_ref, o_ref,
    s1a, s1b, r1a, r1b, s2a, s2b, r2a, r2b, rm1, sm, rm2, gs,
    send1, recv1, send2, recv2, send_m, recv_m, send_g, recv_g,
    got, n_sum, o_sum, send_h, recv_h,
):
    me, group = lax.axis_index("seq"), lax.axis_index("head")
    pairs = peers // 2
    k, j = me // 2, me % 2
    partner = {"seq": me + 1 - 2 * j}
    unroll = pairs <= 4
    bf16 = jnp.bfloat16

    def remote(source, target, here, there, to):
        return pltpu.make_async_remote_copy(
            src_ref=source, dst_ref=target, send_sem=here, recv_sem=there,
            device_id=to, device_id_type=MESH,
        )

    def loop(count, body):
        if unroll:
            for t in range(count):
                body(t)
        else:
            pl.loop(0, count)(body)

    barrier = pltpu.get_barrier_semaphore()
    pl.semaphore_signal(barrier, inc=1, device_id=partner, device_id_type=MESH)

    def greet(t):
        to = {"seq": 2 * ((k + 1 + t) % pairs) + j}
        pl.semaphore_signal(barrier, inc=1, device_id=to, device_id_type=MESH)

    loop(pairs - 1, greet)
    for t in range(groups - 1):
        to = {"head": (group + 1 + t) % groups}
        pl.semaphore_signal(barrier, inc=1, device_id=to, device_id_type=MESH)
    pl.semaphore_wait(barrier, pairs + groups - 1)

    ways = [{"head": (group + 1 + t) % groups} for t in range(groups - 1)]
    tokens = n_sum.shape[0]

    def rows_of(owner):
        return pl.ds(pl.multiple_of(owner * tokens, tokens), tokens)

    def across(source, target, kind, t):
        return remote(source, target, send_h.at[kind, t], recv_h.at[kind, t], ways[t])

    partials = [
        [
            across(ref.at[rows_of((group + 1 + t) % groups)], got.at[kind, t], kind, t)
            for t in range(groups - 1)
        ]
        for kind, ref in enumerate((back_ref, mix_ref))
    ]
    for copies in partials:
        for copy in copies:
            copy.start()

    def piece(owner):
        a = jnp.dot(rows_ref[owner], right_ref[...], preferred_element_type=jnp.float32)
        b = jnp.dot(left_ref[...], cols_ref[owner], preferred_element_type=jnp.float32)
        return a, b

    def first(t):
        return (
            remote(s1a.at[t], r1a.at[t], send1.at[0, t], recv1.at[0, t], partner),
            remote(s1b.at[t], r1b.at[t], send1.at[1, t], recv1.at[1, t], partner),
        )

    first_minor = remote(minor_ref, rm1, send_m.at[pairs], recv_m.at[pairs], partner)
    first_minor.start()

    def give(t):
        a, b = piece(2 * ((k + 1 + t) % pairs) + 1 - j)
        s1a[t] = a.astype(bf16)
        s1b[t] = b.astype(bf16)
        for copy in first(t):
            copy.start()

    loop(pairs, give)
    first_minor.wait()
    sm[...] = minor_ref[...] + rm1[...]

    def second_minor(t):
        to = {"seq": 2 * ((k + 1 + t) % pairs) + j}
        return remote(sm, rm2.at[t], send_m.at[t], recv_m.at[t], to)

    loop(pairs - 1, lambda t: second_minor(t).start())

    own = rows_of(group)
    for copy in partials[0]:
        copy.wait()
    summed = back_ref[own]
    for t in range(groups - 1):
        summed = summed + got[0, t]
    n_sum[...] = summed
    spread_n = [across(n_sum, n_ref.at[own], 2, t) for t in range(groups - 1)]
    for copy in spread_n:
        copy.start()
    n_ref[own] = summed
    for copy in partials[1]:
        copy.wait()
    summed = mix_ref[own]
    for t in range(groups - 1):
        summed = summed + got[1, t]
    summed = (hidden_ref[own].astype(jnp.float32) + summed).astype(bf16)
    o_sum[...] = summed
    spread_o = [across(o_sum, o_ref.at[own], 3, t) for t in range(groups - 1)]
    for copy in spread_o:
        copy.start()
    o_ref[own] = summed

    def second(t):
        to = {"seq": 2 * ((k + 1 + t) % pairs) + j}
        return (
            remote(s2a.at[t], r2a.at[t], send2.at[0, t], recv2.at[0, t], to),
            remote(s2b.at[t], r2b.at[t], send2.at[1, t], recv2.at[1, t], to),
        )

    def join(t):
        a, b = piece(2 * ((k + 1 + t) % pairs) + j)
        for copy in first(t):
            copy.wait()
        return a + r1a[t].astype(jnp.float32), b + r1b[t].astype(jnp.float32)

    def pass_on(t):
        a, b = join(t)
        s2a[t] = a.astype(bf16)
        s2b[t] = b.astype(bf16)
        for copy in second(t):
            copy.start()

    loop(pairs - 1, pass_on)
    a, b = join(pairs - 1)
    a_ref[...] = a
    b_ref[...] = b

    def collect(t):
        for copy in second(t):
            copy.wait()
        a_ref[...] += r2a[t].astype(jnp.float32)
        b_ref[...] += r2b[t].astype(jnp.float32)

    loop(pairs - 1, collect)
    gs[...] = a_ref[:, side_at:]
    shares = [
        remote(gs, g_ref.at[group], send_g.at[t], recv_g.at[t], {"head": (group + 1 + t) % groups})
        for t in range(groups - 1)
    ]
    for copy in shares:
        copy.start()
    g_ref[group] = gs[...]

    loop(pairs - 1, lambda t: second_minor(t).wait())

    def ordered(q, total):
        slot = (k - q + pairs - 1) % pairs
        value = jnp.where(slot == pairs - 1, sm[...], rm2[jnp.minimum(slot, pairs - 2)])
        return total + value

    m_ref[...] = lax.fori_loop(0, pairs, ordered, jnp.zeros(m_ref.shape, jnp.float32))
    for copy in shares + spread_n + spread_o:
        copy.wait()


def weight_sums_of(normed_in, right, normed_out, cotangent, minor, back, mix, hidden):
    peers, groups = lax.axis_size("seq"), lax.axis_size("head")
    pairs = peers // 2
    length, width = normed_in.shape
    part = width // peers
    inner = normed_out.shape[1]
    side = right.shape[1]
    side_at = side - 128
    rows = normed_in.T.reshape(peers, part, length)
    cols = cotangent.reshape(length, peers, part).transpose(1, 0, 2)
    low, full = jnp.bfloat16, jnp.float32
    aa, bb = (part, side), (inner, part)
    token_part = (length // groups, width)

    def slots(count, shape, dtype):
        return VMEM((count,) + shape, dtype)

    return pl.pallas_call(
        functools.partial(sums_kernel, peers, groups, side_at),
        out_shape=(
            jax.ShapeDtypeStruct(aa, full),
            jax.ShapeDtypeStruct(bb, full),
            jax.ShapeDtypeStruct(minor.shape, full),
            jax.ShapeDtypeStruct((groups, part, 128), full),
            jax.ShapeDtypeStruct(back.shape, full),
            jax.ShapeDtypeStruct(hidden.shape, low),
        ),
        in_specs=[IN_VMEM] * 8,
        out_specs=(IN_VMEM,) * 6,
        scratch_shapes=[
            slots(pairs, aa, low), slots(pairs, bb, low),
            slots(pairs, aa, low), slots(pairs, bb, low),
            slots(pairs - 1, aa, low), slots(pairs - 1, bb, low),
            slots(pairs - 1, aa, low), slots(pairs - 1, bb, low),
            VMEM(minor.shape, full), VMEM(minor.shape, full),
            slots(pairs - 1, minor.shape, full),
            VMEM((part, 128), full),
            DMA((2, pairs)), DMA((2, pairs)), DMA((2, pairs)), DMA((2, pairs)),
            DMA((pairs + 1,)), DMA((pairs + 1,)), DMA((groups,)), DMA((groups,)),
            VMEM((2, groups - 1) + token_part, full), VMEM(token_part, full), VMEM(token_part, low),
            DMA((4, groups - 1)), DMA((4, groups - 1)),
        ],
        compiler_params=pltpu.CompilerParams(
            collective_id=3, has_side_effects=True, vmem_limit_bytes=48 * 2**20
        ),
        cost_estimate=pl.CostEstimate(
            flops=10**9, bytes_accessed=2 * 10**8, transcendentals=0
        ),
        name="weight_sums",
    )(rows, right, normed_out.T, cols, minor, back, mix, hidden)


def head_sum_kernel(groups, x_ref, out_ref, got, total, send, recv):
    me = lax.axis_index("head")
    rows = total.shape[0]
    barrier = pltpu.get_barrier_semaphore()
    peers = [{"head": (me + 1 + t) % groups} for t in range(groups - 1)]
    for to in peers:
        pl.semaphore_signal(barrier, inc=1, device_id=to, device_id_type=MESH)
    pl.semaphore_wait(barrier, groups - 1)

    def remote(source, target, phase, t):
        return pltpu.make_async_remote_copy(
            src_ref=source, dst_ref=target, send_sem=send.at[phase, t], recv_sem=recv.at[phase, t],
            device_id=peers[t], device_id_type=MESH,
        )

    def rows_of(owner):
        return pl.ds(pl.multiple_of(owner * rows, rows), rows)

    gives = [
        remote(x_ref.at[rows_of((me + 1 + t) % groups)], got.at[t], 0, t)
        for t in range(groups - 1)
    ]
    for copy in gives:
        copy.start()
    for copy in gives:
        copy.wait()
    summed = x_ref[rows_of(me)]
    for t in range(groups - 1):
        summed = summed + got[t]
    total[...] = summed
    shares = [remote(total, out_ref.at[rows_of(me)], 1, t) for t in range(groups - 1)]
    for copy in shares:
        copy.start()
    out_ref[rows_of(me)] = summed
    for copy in shares:
        copy.wait()


def head_sum(value):
    groups = lax.axis_size("head")
    part = (value.shape[0] // groups, value.shape[1])
    return pl.pallas_call(
        functools.partial(head_sum_kernel, groups),
        out_shape=jax.ShapeDtypeStruct(value.shape, jnp.float32),
        in_specs=[IN_VMEM],
        out_specs=IN_VMEM,
        scratch_shapes=[
            VMEM((groups - 1,) + part, jnp.float32), VMEM(part, jnp.float32),
            DMA((2, groups - 1)), DMA((2, groups - 1)),
        ],
        compiler_params=pltpu.CompilerParams(collective_id=4, has_side_effects=True),
        cost_estimate=pl.CostEstimate(
            flops=10**6, bytes_accessed=3 * 10**7, transcendentals=0
        ),
        name="head_sum",
    )(value)


def on_device(
    hidden,
    cotangent,
    pre_gain,
    w_zx,
    w_bc,
    w_dt,
    conv_x_w,
    conv_x_b,
    conv_bc_w,
    conv_bc_b,
    dt_bias,
    a_log,
    d_skip,
    gate_gain,
    w_out,
):
    seq_count, length, _ = hidden.shape
    head_count = dt_bias.shape[0]
    inner_dev = w_zx.shape[2]
    head_size = inner_dev // head_count
    states = w_bc.shape[1] // 2
    conv_reach = conv_x_w.shape[0] - 1
    full_inner = inner_dev * lax.axis_size("head")
    residual = hidden.astype(jnp.float32)
    in_rstd = lax.rsqrt(jnp.mean(residual * residual, axis=-1, keepdims=True) + EPSILON)
    normed_in = (residual * in_rstd * pre_gain).astype(jnp.bfloat16)
    projected = jnp.einsum("std,dke->stke", normed_in, w_zx, preferred_element_type=jnp.float32)
    gating = projected[:, :, 0]
    conv_in = projected[:, :, 1].astype(jnp.bfloat16)
    bc_in = jnp.einsum("std,dn->stn", normed_in, w_bc, preferred_element_type=jnp.float32).astype(
        jnp.bfloat16
    )
    dt_raw = jnp.einsum("std,dh->sth", normed_in, w_dt, preferred_element_type=jnp.float32)
    edge_x, edge_bc = from_behind(
        (conv_in[:, length - conv_reach :], bc_in[:, length - conv_reach :]), "seq", 1
    )
    ext_x = jnp.concatenate([edge_x, conv_in], 1).astype(jnp.float32)
    ext_bc = jnp.concatenate([edge_bc, bc_in], 1).astype(jnp.float32)
    pre_x = conv_apply(ext_x, conv_x_w, conv_x_b, length)
    pre_bc = conv_apply(ext_bc, conv_bc_w, conv_bc_b, length)
    x_heads = kept_low(jax.nn.silu(pre_x)).reshape(seq_count, length, head_count, head_size)
    bc_post = jax.nn.silu(pre_bc)
    b_mat = kept_low(bc_post[:, :, :states])
    c_mat = kept_low(bc_post[:, :, states:])
    deltas = jax.nn.softplus(dt_raw + dt_bias)
    rates = -jnp.exp(a_log)
    log_decay = deltas * rates
    cumulative = jnp.cumsum(log_decay, axis=1)
    last_cum = cumulative[:, -1]
    block_decay = jnp.exp(last_cum)
    tail_exp = jnp.exp(last_cum[:, None] - cumulative)
    tail_w = tail_exp * deltas
    weighted_x = tail_w[..., None] * x_heads
    local_state = jnp.einsum("sthp,stn->shpn", weighted_x, b_mat, precision=HIGHEST)
    incoming = state_scan(block_decay[0], local_state[0], False)[None]
    scores = jnp.einsum("stn,sun->stu", c_mat, b_mat, precision=HIGHEST)
    row_ids = lax.broadcasted_iota(jnp.int32, (length, length), 0)
    column_ids = lax.broadcasted_iota(jnp.int32, (length, length), 1)
    causal = (row_ids >= column_ids)[None, :, :, None]
    spread = cumulative[:, :, None, :] - cumulative[:, None, :, :]
    decays = jnp.where(causal, jnp.exp(jnp.where(causal, spread, 0.0)), 0.0)
    weights = scores[..., None] * decays * deltas[:, None, :, :]
    inside = jnp.einsum("stuh,suhp->sthp", weights, x_heads, precision=HIGHEST)
    growth = jnp.exp(cumulative)
    from_state = jnp.einsum("stn,shpn->sthp", c_mat, incoming, precision=HIGHEST)
    outside = growth[..., None] * from_state
    ssd_out = inside + outside + d_skip[:, None] * x_heads
    flat_ssd = ssd_out.reshape(seq_count, length, inner_dev)
    gate_act = jax.nn.silu(gating)
    gated = flat_ssd * gate_act
    grad_normed = jnp.einsum("std,ed->ste", cotangent, w_out, preferred_element_type=jnp.float32)
    scaled_out = grad_normed * gate_gain
    squares, dotted = lax.psum(
        jnp.stack([jnp.sum(gated * gated, axis=-1), jnp.sum(scaled_out * gated, axis=-1)]), "head"
    )
    gate_rstd = lax.rsqrt(squares / full_inner + EPSILON)[..., None]
    normed_out = (gated * gate_rstd * gate_gain).astype(jnp.bfloat16)
    partial_value = jnp.einsum("ste,ed->std", normed_out, w_out, preferred_element_type=jnp.float32)
    grad_gate_gain = jnp.sum(grad_normed * gated * gate_rstd, axis=(0, 1))
    grad_gated = gate_rstd * scaled_out - gated * gate_rstd**3 * (dotted / full_inner)[..., None]
    grad_ssd = (grad_gated * gate_act).reshape(seq_count, length, head_count, head_size)
    grad_gating = grad_gated * flat_ssd * silu_slope(gating)
    grad_d_skip = jnp.sum(grad_ssd * x_heads, axis=(0, 1, 3))
    grad_x = d_skip[:, None] * grad_ssd
    grad_from = growth[..., None] * grad_ssd
    grad_cum = jnp.sum(grad_ssd * outside, axis=-1)
    state_grad_local = jnp.einsum("sthp,stn->shpn", grad_from, c_mat, precision=HIGHEST)
    grad_c = jnp.einsum("sthp,shpn->stn", grad_from, incoming, precision=HIGHEST)
    after = state_scan(block_decay[0], state_grad_local[0], True)[None]
    grad_last = jnp.sum(after * incoming, axis=(2, 3)) * block_decay
    grad_weighted = jnp.einsum("shpn,stn->sthp", after, b_mat, precision=HIGHEST)
    grad_b = jnp.einsum("sthp,shpn->stn", weighted_x, after, precision=HIGHEST)
    grad_x = grad_x + tail_w[..., None] * grad_weighted
    grad_tail = jnp.sum(grad_weighted * x_heads, axis=-1)
    grad_last = grad_last + jnp.sum(grad_tail * tail_w, axis=1)
    grad_cum = grad_cum - grad_tail * tail_w
    grad_deltas = grad_tail * tail_exp
    grad_weights = jnp.einsum("sthp,suhp->stuh", grad_ssd, x_heads, precision=HIGHEST)
    grad_x = grad_x + jnp.einsum("stuh,sthp->suhp", weights, grad_ssd, precision=HIGHEST)
    grad_scores = jnp.sum(grad_weights * decays * deltas[:, None, :, :], axis=-1)
    exponent_grad = grad_weights * weights
    grad_cum = grad_cum + jnp.sum(exponent_grad, axis=2) - jnp.sum(exponent_grad, axis=1)
    grad_deltas = grad_deltas + jnp.sum(grad_weights * scores[..., None] * decays, axis=1)
    grad_c = grad_c + jnp.einsum("stu,sun->stn", grad_scores, b_mat, precision=HIGHEST)
    grad_b = grad_b + jnp.einsum("stu,stn->sun", grad_scores, c_mat, precision=HIGHEST)
    grad_cum = grad_cum.at[:, -1].add(grad_last)
    grad_log_decay = jnp.flip(jnp.cumsum(jnp.flip(grad_cum, 1), axis=1), 1)
    grad_a_log = rates * jnp.sum(grad_log_decay * deltas, axis=(0, 1))
    grad_u = (grad_deltas + grad_log_decay * rates) * jax.nn.sigmoid(dt_raw + dt_bias)
    grad_dt_bias = jnp.sum(grad_u, axis=(0, 1))
    grad_dt_raw = grad_u.astype(jnp.bfloat16)
    grad_bc_post = head_sum(jnp.concatenate([grad_b[0], grad_c[0]], -1))[None]
    grad_pre_x = grad_x.reshape(seq_count, length, inner_dev) * silu_slope(pre_x)
    grad_pre_bc = grad_bc_post * silu_slope(pre_bc)
    grad_conv_x_w, grad_conv_x_b, grad_ext_x = conv_reverse(ext_x, conv_x_w, grad_pre_x, length)
    grad_conv_bc_w, grad_conv_bc_b, grad_ext_bc = conv_reverse(
        ext_bc, conv_bc_w, grad_pre_bc, length
    )
    sent_x, sent_bc = from_behind(
        (grad_ext_x[:, :conv_reach], grad_ext_bc[:, :conv_reach]), "seq", -1
    )
    tail_pad = ((0, 0), (length - conv_reach, 0), (0, 0))
    grad_conv_in = grad_ext_x[:, conv_reach:] + jnp.pad(sent_x, tail_pad)
    grad_bc_in = (grad_ext_bc[:, conv_reach:] + jnp.pad(sent_bc, tail_pad)).astype(jnp.bfloat16)
    grad_projected = jnp.concatenate([grad_gating, grad_conv_in], -1).astype(jnp.bfloat16)
    head_part = jnp.einsum(
        "ste,de->std",
        grad_projected,
        w_zx.reshape(w_zx.shape[0], 2 * inner_dev),
        preferred_element_type=jnp.float32,
    )
    head_part = head_part + jnp.einsum(
        "sth,dh->std", grad_dt_raw, w_dt, preferred_element_type=jnp.float32
    )
    groups = lax.axis_size("head")
    share = w_bc.shape[1] // groups
    group_at = lax.axis_index("head") * share
    group_bc = lax.dynamic_slice_in_dim(grad_bc_in, group_at, share, axis=2)
    head_part = head_part + jnp.einsum(
        "stn,dn->std",
        group_bc,
        lax.dynamic_slice_in_dim(w_bc, group_at, share, axis=1),
        preferred_element_type=jnp.float32,
    )
    side = jnp.concatenate([group_bc[0], grad_dt_raw[0]], -1)
    spare = jnp.zeros((length, 128 - share - head_count), jnp.bfloat16)
    right = jnp.concatenate([grad_projected[0], side, spare], -1)
    minor = (
        grad_conv_x_w,
        grad_conv_x_b,
        grad_conv_bc_w,
        grad_conv_bc_b,
        grad_gate_gain,
        grad_dt_bias,
        grad_a_log,
        grad_d_skip,
    )
    flat = jnp.concatenate([part.reshape(-1) for part in minor])
    flat = jnp.pad(flat, (0, -flat.size % 1024)).reshape(-1, 128)
    side_sum, out_sum, minor_sum, shared, back_sum, output = weight_sums_of(
        normed_in[0],
        right,
        normed_out[0],
        cotangent[0],
        flat,
        head_part[0],
        partial_value[0],
        hidden[0],
    )
    grad_normed_in = back_sum[None]
    grad_pre_gain = jnp.sum(grad_normed_in * residual * in_rstd, axis=(0, 1))
    scaled_in = grad_normed_in * pre_gain
    grad_hidden = (
        cotangent.astype(jnp.float32)
        + in_rstd * scaled_in
        - residual * in_rstd**3 * jnp.mean(scaled_in * residual, axis=-1, keepdims=True)
    )
    line, minor_sums, at = minor_sum.reshape(-1), [], 0
    for part in minor:
        minor_sums.append(line[at : at + part.size].reshape(part.shape))
        at += part.size
    rows_here = side_sum.shape[0]
    sum_zx = side_sum[:, : 2 * inner_dev].reshape(rows_here, 2, inner_dev)
    sum_dt = side_sum[:, 2 * inner_dev + share : 2 * inner_dev + share + head_count]
    sum_bc = shared[:, :, :share].transpose(1, 0, 2).reshape(rows_here, groups * share)
    return (
        output[None],
        grad_hidden,
        lax.psum(grad_pre_gain, "seq"),
        sum_zx,
        sum_bc,
        sum_dt,
        minor_sums[0],
        minor_sums[1],
        minor_sums[2],
        minor_sums[3],
        minor_sums[5],
        minor_sums[6],
        minor_sums[7],
        minor_sums[4],
        out_sum,
    )


def solution(mesh):
    return jax.shard_map(
        on_device,
        mesh=mesh,
        in_specs=(
            P(None, "seq", None),
            P(None, "seq", None),
            P(),
            P(None, None, "head"),
            P(),
            P(None, "head"),
            P(None, "head"),
            P("head"),
            P(),
            P(),
            P("head"),
            P("head"),
            P("head"),
            P("head"),
            P("head", None),
        ),
        out_specs=(
            P(None, "seq", None),
            P(None, "seq", None),
            P(),
            P("seq", None, "head"),
            P("seq", None),
            P("seq", "head"),
            P(None, "head"),
            P("head"),
            P(),
            P(),
            P("head"),
            P("head"),
            P("head"),
            P("head"),
            P("head", "seq"),
        ),
        check_vma=False,
    )
```
